32 devices in a mesh: head: 4 (over y, core), seq: 8 (over z, x).
Axes of the slice: x: 2, y: 2, z: 4, core: 2. Of those that a mesh axis runs over, the one named last changes fastest.
Arguments:
- queries: bfloat16 [4096, 4096], P('seq', 'head'), may hold values from -6 to 6
- keys: bfloat16 [4096, 4096], P('seq', 'head'), may hold values from -6 to 6
- values: bfloat16 [4096, 4096], P('seq', 'head'), may hold values from -6 to 6
- rate: float32 [8, 4096], P('head', 'seq'), may hold values from 0.0001 to 0.001
- fast_gate: float32 [8, 512, 512], P('head', 'seq'), may hold values from -3 to 3
- fast_up: float32 [8, 512, 512], P('head', 'seq'), may hold values from -3 to 3
- fast_down: float32 [8, 512, 512], P('head', 'seq'), may hold values from -8 to 8
- out_gain: float32 [4096], P('head'), may hold values from 0.25 to 1.75
Outputs:
- mixed: bfloat16 [4096, 4096], P('seq', 'head')
- new_gate: float32 [8, 512, 512], P('head', 'seq')
- new_up: float32 [8, 512, 512], P('head', 'seq')
- new_down: float32 [8, 512, 512], P('head', 'seq')
The draws below stay inside these ranges and needn't reach their ends.
All inputs are finite; a program needn't handle non-finite values.
Results may differ from the reference program's by a relative error of at most 0.012.
Values may be sent and summed in bfloat16 or wider, within the bound.
A program may use at most 128 MiB of HBM per device.

```python
import math
import jax
import jax.numpy as jnp
from jax import lax

HEADS = 8
HD = 512
FAST = 512
WINDOW = 512
GROUP = 4096


def query_key_pair(key):
    key_q, key_k = jax.random.split(jax.random.fold_in(key, 7), 2)
    width = HEADS * HD
    q_vals = 1.3 * jax.random.truncated_normal(key_q, -4.0, 4.0, (GROUP, width), jnp.float32)
    k_vals = 1.3 * jax.random.truncated_normal(key_k, -4.0, 4.0, (GROUP, width), jnp.float32)
    return (q_vals, k_vals)


def draw_queries(key, part):
    return query_key_pair(key)[0].astype(jnp.bfloat16)


def draw_keys(key, part):
    return query_key_pair(key)[1].astype(jnp.bfloat16)


def fast_matrix(key, salt, rows_n, cols_n, rising):
    key_base, key_cols = jax.random.split(jax.random.fold_in(key, salt))
    base = jax.random.truncated_normal(key_base, -4.0, 4.0, (HEADS, rows_n, cols_n), jnp.float32)
    row_scale = 10.0 ** (jnp.arange(rows_n, dtype=jnp.float32) / (rows_n - 1))
    col_scale = jnp.exp(jax.random.uniform(key_cols, (HEADS, 1, cols_n), jnp.float32, 0.0, math.log(10.0)))
    overall = jnp.sqrt(jnp.mean(row_scale * row_scale) * jnp.mean(col_scale * col_scale))
    if rising:
        head_scale = jnp.exp(jnp.arange(HEADS, dtype=jnp.float32) / max(HEADS - 1, 1) * math.log(3.0))
    else:
        head_scale = jnp.ones((HEADS,), jnp.float32)
    result = base * row_scale[None, :, None] * col_scale / overall / math.sqrt(rows_n)
    return (result * head_scale[:, None, None]).astype(jnp.float32)


def draw_fast_gate(key, part):
    return fast_matrix(key, 11, HD, FAST, False)


def draw_fast_up(key, part):
    return fast_matrix(key, 13, HD, FAST, False)


def draw_fast_down(key, part):
    return fast_matrix(key, 17, FAST, HD, True)


def block_scale(key, extent, cuts, least, high):
    loudness, own = 1.0, jax.random.fold_in(key, 6)
    for dim, blocks in cuts:
        heights = jnp.exp(jax.random.uniform(jax.random.fold_in(own, dim), (blocks,), jnp.float32, least / len(cuts), high / len(cuts)))
        loudness = loudness * jnp.repeat(heights, extent[dim] // blocks).reshape([-1 if axis == dim else 1 for axis in range(len(extent))])
    return loudness


def centred(key, dims, deviation, limit, cuts=(), kind=jnp.bfloat16):
    loudness = block_scale(key, dims, cuts, -0.22, 0.18) if cuts else 1.0
    values = jax.random.normal(key, dims, jnp.float32) * deviation * loudness
    return jnp.minimum(jnp.maximum(values, -limit), limit).astype(kind)


def setup_inputs(seed: int = 0) -> dict:
    key_list = jax.random.split(jax.random.key(seed), 9)
    return {
        "queries": draw_queries(jax.random.fold_in(key_list[8], 71), 0),
        "keys": draw_keys(jax.random.fold_in(key_list[8], 71), 0),
        "values": centred(key_list[2], (GROUP, HEADS * HD), 1.0, 6.0, ((0, 8), (1, 4))),
        "rate": jnp.clip(jnp.exp(math.log(0.001) - 2.3025852 * jax.random.uniform(key_list[3], (HEADS, GROUP), jnp.float32) ** block_scale(key_list[3], (HEADS, GROUP), ((0, 4), (1, 8)), -0.2, 0.2)), 0.0001, 0.001),
        "fast_gate": draw_fast_gate(jax.random.fold_in(key_list[8], 71), 0),
        "fast_up": draw_fast_up(jax.random.fold_in(key_list[8], 71), 0),
        "fast_down": draw_fast_down(jax.random.fold_in(key_list[8], 71), 0),
        "out_gain": jnp.clip(1.0 + 0.15 * jax.random.normal(key_list[7], (HEADS * HD,), jnp.float32), 0.25, 1.75),
    }


EPS = 1e-06

def rescale(old, upd):
    old_sq = lax.optimization_barrier(jnp.sum(old * old, axis=0))
    new_sq = lax.optimization_barrier(jnp.sum(upd * upd, axis=0))
    return upd * (jnp.sqrt(old_sq) / jnp.sqrt(new_sq + EPS))[None, :]

def head_update(inputs):
    qh, kh, vh, eta, w_one, w_three, w_two = inputs
    w1b = w_one.astype(jnp.bfloat16)
    w3b = w_three.astype(jnp.bfloat16)
    w2b = w_two.astype(jnp.bfloat16)
    pre_a = jnp.dot(kh, w1b, preferred_element_type=jnp.float32)
    pre_b = jnp.dot(kh, w3b, preferred_element_type=jnp.float32)
    sigma = jax.nn.sigmoid(pre_a)
    hidden = (pre_a * sigma * pre_b).astype(jnp.bfloat16)
    scaled = (eta[:, None] * vh.astype(jnp.float32)).astype(jnp.bfloat16)
    grad_two = jnp.dot(hidden.T, scaled, preferred_element_type=jnp.float32)
    back = jnp.dot(scaled, w2b.T, preferred_element_type=jnp.float32)
    d_gate = (back * pre_b * sigma * (1.0 + pre_a * (1.0 - sigma))).astype(jnp.bfloat16)
    d_up = (back * pre_a * sigma).astype(jnp.bfloat16)
    grad_one = jnp.dot(kh.T, d_gate, preferred_element_type=jnp.float32)
    grad_three = jnp.dot(kh.T, d_up, preferred_element_type=jnp.float32)
    new_one = rescale(w_one, w_one + grad_one)
    new_three = rescale(w_three, w_three + grad_three)
    new_two = rescale(w_two, w_two + grad_two)
    apply_a = jnp.dot(qh, new_one.astype(jnp.bfloat16), preferred_element_type=jnp.float32)
    apply_b = jnp.dot(qh, new_three.astype(jnp.bfloat16), preferred_element_type=jnp.float32)
    apply_h = (apply_a * jax.nn.sigmoid(apply_a) * apply_b).astype(jnp.bfloat16)
    result = jnp.dot(apply_h, new_two.astype(jnp.bfloat16), preferred_element_type=jnp.float32)
    return (result, new_one, new_three, new_two)

def reference(queries, keys, values, rate, fast_gate, fast_up, fast_down, out_gain):
    q_three = queries.reshape(GROUP, HEADS, HD)
    k_three = keys.reshape(GROUP, HEADS, HD)
    v_three = values.reshape(GROUP, HEADS, HD)
    lead = jnp.zeros((WINDOW, HEADS, HD), jnp.bfloat16)
    padded_k = jnp.concatenate([lead, k_three], axis=0)
    padded_v = jnp.concatenate([lead, v_three], axis=0)
    scale = 1.0 / math.sqrt(HD)
    rows_i = jnp.arange(WINDOW, dtype=jnp.int32)[:, None]
    cols_j = jnp.arange(2 * WINDOW, dtype=jnp.int32)[None, :]

    def attend(block):
        start = (block * WINDOW).astype(jnp.int32)
        q_blk = lax.dynamic_slice_in_dim(q_three, start, WINDOW, 0).astype(jnp.float32)
        k_blk = lax.dynamic_slice_in_dim(padded_k, start, 2 * WINDOW, 0).astype(jnp.float32)
        v_blk = lax.dynamic_slice_in_dim(padded_v, start, 2 * WINDOW, 0).astype(jnp.float32)
        scores = jnp.einsum('qhd,khd->hqk', q_blk, k_blk) * scale
        valid = (cols_j > rows_i) & (cols_j <= rows_i + WINDOW) & (start + cols_j >= WINDOW)
        scores = jnp.where(valid[None], scores, -jnp.inf)
        top = lax.optimization_barrier(jnp.max(scores, axis=-1, keepdims=True))
        expo = jnp.exp(scores - top)
        probs = (expo / lax.optimization_barrier(jnp.sum(expo, axis=-1, keepdims=True))).astype(jnp.bfloat16)
        return jnp.einsum('hqk,khd->qhd', probs.astype(jnp.float32), v_blk)
    attn = lax.map(attend, jnp.arange(GROUP // WINDOW, dtype=jnp.int32)).reshape(GROUP, HEADS, HD)
    result, new_gate, new_up, new_down = lax.map(head_update, (q_three.transpose(1, 0, 2), k_three.transpose(1, 0, 2), v_three.transpose(1, 0, 2), rate, fast_gate, fast_up, fast_down))
    branch = result.transpose(1, 0, 2)
    mean_sq = lax.optimization_barrier(jnp.mean(branch * branch, axis=(1, 2)))
    inv = lax.rsqrt(mean_sq + EPS)
    gain = out_gain.reshape(HEADS, HD)
    mixed = (attn + branch * inv[:, None, None] * gain[None]).astype(jnp.bfloat16)
    return (mixed.reshape(GROUP, HEADS * HD), new_gate, new_up, new_down)
```

```python
import functools
import math

import jax
import jax.numpy as jnp
from jax import lax
from jax.experimental import pallas as pl
from jax.experimental.pallas import tpu as pltpu
from jax.sharding import PartitionSpec as P

WINDOW = 512
EPS = 1e-06
TILE = 128
MESH = pl.DeviceIdType.MESH
F32 = jnp.float32
BF16 = jnp.bfloat16


def dot(a, b):
    return jnp.dot(a, b, preferred_element_type=F32)


def dot_lhs_t(a, b):
    return lax.dot_general(a, b, (((0,), (0,)), ((), ())), preferred_element_type=F32)


def dot_rhs_t(a, b):
    return lax.dot_general(a, b, (((1,), (1,)), ((), ())), preferred_element_type=F32)


def kernel(
    n, hn,
    q, k, v, rate, gain, w1, w3, w2,
    mixed, o1, o3, o2,
    wg, ug, pg, rs_out, rs_in, own, kx, vx, gv, hid, dab, attn, branch, sq, sq_in,
    ag_s, ag_r, rs_s, rs_r, au_s, au_r, halo_s, halo_r, sq_s, sq_r,
):
    rows, width = q.shape
    heads, shard, hd = w1.shape
    fast = w1.shape[2]
    half = n // 2
    me = lax.axis_index("seq")
    hme = lax.axis_index("head")
    odd = lax.rem(me, 2)
    pos = (1 - odd) * lax.div(me, 2) + odd * (n - lax.div(me + 1, 2))

    def at_pos(p):
        p = lax.rem(p + 2 * n, n)
        back = lax.div(p, half)
        return (1 - back) * 2 * p + back * (2 * (n - p) - 1)

    neighbour = (at_pos(pos + 1), at_pos(pos - 1))
    sign = (1, -1)
    after, before = lax.rem(me + 1, n), lax.rem(me + n - 1, n)

    barrier = pltpu.get_barrier_semaphore()
    for s in (neighbour[0], neighbour[1], after, before):
        pl.semaphore_signal(barrier, inc=1, device_id={"seq": s}, device_id_type=MESH)
    for d in range(1, hn):
        pl.semaphore_signal(
            barrier, inc=1, device_id={"head": lax.rem(hme + d, hn)}, device_id_type=MESH
        )
    for h in range(heads):
        for m, w in enumerate((w1, w3, w2)):
            wg[h, me, m] = w[h].astype(BF16)
    pl.semaphore_wait(barrier, 4 + hn - 1)

    sent = []

    def carries(h, d):
        return h % 2 == d

    def gather_send(buf, ss, rr, h, s):
        for d in range(2):
            if s == half and not carries(h, d):
                continue
            owner = at_pos(pos - sign[d] * (s - 1))
            if s > 1:
                gather_wait(buf, ss, rr, h, s - 1, d)
            block = buf.at[h, owner]
            c = pltpu.make_async_remote_copy(
                src_ref=block, dst_ref=block,
                send_sem=ss.at[d, h, s - 1], recv_sem=rr.at[d, h, s - 1],
                device_id={"seq": neighbour[d]}, device_id_type=MESH,
            )
            c.start()
            sent.append(c)

    def gather_wait(buf, ss, rr, h, s, d):
        owner = at_pos(pos - sign[d] * s)
        block = buf.at[h, owner]
        pltpu.make_async_remote_copy(
            src_ref=block, dst_ref=block,
            send_sem=ss.at[d, h, s - 1], recv_sem=rr.at[d, h, s - 1],
            device_id={"seq": neighbour[d]}, device_id_type=MESH,
        ).wait_recv()

    def gather_finish(buf, ss, rr, h):
        for d in range(2):
            if carries(h, d):
                gather_wait(buf, ss, rr, h, half, d)
            elif half > 1:
                gather_wait(buf, ss, rr, h, half - 1, d)

    def rs_copy(h, s, d):
        return pltpu.make_async_remote_copy(
            src_ref=rs_out.at[d, h, s - 1], dst_ref=rs_in.at[d, h, s - 1],
            send_sem=rs_s.at[d, h, s - 1], recv_sem=rs_r.at[d, h, s - 1],
            device_id={"seq": neighbour[d]}, device_id_type=MESH,
        )

    def reduce_send(h, s):
        for d in range(2):
            if s == 1 and not carries(h, d):
                continue
            target = at_pos(pos + sign[d] * (half - s + 1))
            part = pg[h, target]
            if s > 2 or (s == 2 and carries(h, d)):
                rs_copy(h, s - 1, d).wait_recv()
                part = part + rs_in[d, h, s - 2].astype(F32)
            rs_out[d, h, s - 1] = part.astype(BF16)
            c = rs_copy(h, s, d)
            c.start()
            sent.append(c)

    def reduce_finish(h):
        total = pg[h, me]
        for d in range(2):
            if half > 1 or carries(h, d):
                rs_copy(h, half, d).wait_recv()
                total = total + rs_in[d, h, half - 1].astype(F32)
        for m, w in enumerate((w1, w3, w2)):
            upd = w[h] + total[m]
            own[h, m] = upd
            ug[h, me, m] = upd.astype(BF16)

    def cols(h):
        return slice(h * hd, (h + 1) * hd)

    halo = []
    for h in range(heads):
        for j, (src, dst) in enumerate(((k, kx), (v, vx))):
            halo.append(pltpu.make_async_remote_copy(
                src_ref=src.at[rows - WINDOW:rows, cols(h)], dst_ref=dst.at[0:WINDOW, cols(h)],
                send_sem=halo_s.at[h, j], recv_sem=halo_r.at[h, j],
                device_id={"seq": after}, device_id_type=MESH,
            ))

    def halo_send(h):
        @pl.when(me < n - 1)
        def _():
            for j in range(2):
                halo[2 * h + j].start()

    def halo_wait(h):
        @pl.when(me > 0)
        def _():
            for j in range(2):
                halo[2 * h + j].wait_recv()

    def column(row):
        return jnp.transpose(jnp.broadcast_to(row, (TILE, row.shape[1])))

    def prepare(h):
        eta = column(rate[h:h + 1, :])[:, :1]
        gv[h] = (eta * v[:, cols(h)].astype(F32)).astype(BF16)

    def full(buf, h, m):
        return buf[h, :, m].reshape(n * shard, hd)

    def tiles(body):
        @pl.loop(0, rows // TILE)
        def _(i):
            body(pl.ds(pl.multiple_of(i * TILE, TILE), TILE))

    def gradients(h):
        @tiles
        def _(at):
            kt, gt = k[at, cols(h)], gv[h, at]
            a = dot(kt, full(wg, h, 0))
            b = dot(kt, full(wg, h, 1))
            back = dot_rhs_t(gt, full(wg, h, 2))
            g = jax.nn.sigmoid(a)
            ag = a * g
            hid[at, :] = (ag * b).astype(BF16)
            dab[at, :fast] = (back * b * g * (1.0 + a * (1.0 - g))).astype(BF16)
            dab[at, fast:] = (back * ag).astype(BF16)

        kh = k[:, cols(h)]
        for m in range(2):
            pg[h, :, m] = dot_lhs_t(kh, dab[:, m * fast:(m + 1) * fast]).reshape(n, shard, fast)
        pg[h, :, 2] = dot_lhs_t(hid[...], gv[h]).reshape(n, shard, hd)

    def attention(h):
        span = WINDOW + TILE
        @pl.loop(0, rows // TILE)
        def _(i):
            start = pl.multiple_of(i * TILE, TILE)
            s = dot_rhs_t(q[pl.ds(start, TILE), cols(h)], kx[pl.ds(start, span), cols(h)])
            s = s * (1.0 / math.sqrt(hd))
            r = lax.broadcasted_iota(jnp.int32, (TILE, span), 0)
            c = lax.broadcasted_iota(jnp.int32, (TILE, span), 1)
            ok = (c > r) & (c <= r + WINDOW) & (start + c + me * rows >= WINDOW)
            s = jnp.where(ok, s, -jnp.inf)
            e = jnp.exp(s - jnp.max(s, axis=1, keepdims=True))
            p = (e * (1.0 / jnp.sum(e, axis=1, keepdims=True))).astype(BF16)
            attn[h, pl.ds(start, TILE), :] = dot(p, vx[pl.ds(start, span), cols(h)])

    def sum_squares(buf, h, m):
        x = full(buf, h, m).astype(F32)
        return jnp.sum(x * x, axis=0, keepdims=True)

    def apply(h):
        ratio = []
        for m, out in enumerate((o1, o3, o2)):
            old, new = sum_squares(wg, h, m), sum_squares(ug, h, m)
            ratio.append(jnp.sqrt(old) / jnp.sqrt(new + EPS))
            out[h] = own[h, m] * ratio[m]

        @tiles
        def _(at):
            qt = q[at, cols(h)]
            a = dot(qt, full(ug, h, 0)) * ratio[0]
            b = dot(qt, full(ug, h, 1)) * ratio[1]
            hh = (a * jax.nn.sigmoid(a) * b).astype(BF16)
            f = dot(hh, full(ug, h, 2)) * ratio[2]
            branch[h, at, :] = f
            row_sq = jnp.broadcast_to(jnp.sum(f * f, axis=1, keepdims=True), (TILE, TILE))
            flat = jnp.transpose(row_sq)[:8]
            if h == 0:
                sq[:, at] = flat
            else:
                sq[:, at] = sq[:, at] + flat

    for h in range(heads):
        gather_send(wg, ag_s, ag_r, h, 1)
    for src, dst in ((k, kx), (v, vx)):
        dst[WINDOW:, :] = src[...]

    @pl.when(me == 0)
    def _():
        for dst in (kx, vx):
            dst[:WINDOW, :] = jnp.zeros((WINDOW, width), BF16)

    for h in range(heads):
        prepare(h)
    for s in range(2, half + 1):
        for h in range(heads):
            gather_send(wg, ag_s, ag_r, h, s)
    halo_send(0)
    for h in range(heads):
        gather_finish(wg, ag_s, ag_r, h)
        gradients(h)
        reduce_send(h, 1)
    halo_wait(0)
    for h in range(heads):
        if h > 0:
            halo_send(h)
    for s in range(2, half + 1):
        for h in range(heads):
            reduce_send(h, s)
        if s == 2:
            attention(0)
    for h in range(heads):
        reduce_finish(h)
        gather_send(ug, au_s, au_r, h, 1)
    for h in range(1, heads):
        halo_wait(h)
        attention(h)
    for s in range(2, half + 1):
        for h in range(heads):
            gather_send(ug, au_s, au_r, h, s)
    for h in range(heads):
        gather_finish(ug, au_s, au_r, h)
        apply(h)

    mine = []
    for d in range(1, hn):
        c = pltpu.make_async_remote_copy(
            src_ref=sq, dst_ref=sq_in.at[d - 1],
            send_sem=sq_s.at[d - 1], recv_sem=sq_r.at[d - 1],
            device_id={"head": lax.rem(hme + d, hn)}, device_id_type=MESH,
        )
        c.start()
        mine.append(c)
    for c in sent:
        c.wait_send()

    @pl.when(me < n - 1)
    def _():
        for c in halo:
            c.wait_send()

    total = sq[...]
    for d, c in enumerate(mine):
        c.wait_recv()
        total = total + sq_in[d]
    for c in mine:
        c.wait_send()
    sq[...] = lax.rsqrt(total * (1.0 / (hn * width)) + EPS)

    @tiles
    def _(at):
        inv = column(sq[0:1, at])[:, :1]
        for h in range(heads):
            f = branch[h, at, :] * inv * gain[:, cols(h)]
            mixed[at, cols(h)] = (attn[h, at, :] + f).astype(BF16)


def local(n, hn, queries, keys, values, rate, fast_gate, fast_up, fast_down, out_gain):
    rows, width = queries.shape
    heads, shard, hd = fast_gate.shape
    half = n // 2
    piece = (3, shard, hd)
    dma = pltpu.SemaphoreType.DMA
    vmem = pl.BlockSpec(memory_space=pltpu.VMEM)
    return pl.pallas_call(
        functools.partial(kernel, n, hn),
        out_shape=(
            jax.ShapeDtypeStruct((rows, width), BF16),
            jax.ShapeDtypeStruct(fast_gate.shape, F32),
            jax.ShapeDtypeStruct(fast_up.shape, F32),
            jax.ShapeDtypeStruct(fast_down.shape, F32),
        ),
        in_specs=[vmem] * 8,
        out_specs=(vmem,) * 4,
        scratch_shapes=[
            pltpu.VMEM((heads, n) + piece, BF16),
            pltpu.VMEM((heads, n) + piece, BF16),
            pltpu.VMEM((heads, n) + piece, F32),
            pltpu.VMEM((2, heads, half) + piece, BF16),
            pltpu.VMEM((2, heads, half) + piece, BF16),
            pltpu.VMEM((heads,) + piece, F32),
            pltpu.VMEM((WINDOW + rows, width), BF16),
            pltpu.VMEM((WINDOW + rows, width), BF16),
            pltpu.VMEM((heads, rows, hd), BF16),
            pltpu.VMEM((rows, hd), BF16),
            pltpu.VMEM((rows, 2 * hd), BF16),
            pltpu.VMEM((heads, rows, hd), F32),
            pltpu.VMEM((heads, rows, hd), F32),
            pltpu.VMEM((8, rows), F32),
            pltpu.VMEM((hn - 1, 8, rows), F32),
        ]
        + [dma((2, heads, half))] * 6
        + [dma((heads, 2))] * 2
        + [dma((hn - 1,))] * 2,
        compiler_params=pltpu.CompilerParams(
            collective_id=0, has_side_effects=True, vmem_limit_bytes=60 * 1024 * 1024
        ),
        name="ttt_layer",
    )(queries, keys, values, rate, out_gain.reshape(1, width), fast_gate, fast_up, fast_down)


def solution(mesh):
    weights = P("head", "seq", None)
    tokens = P("seq", "head")
    return jax.shard_map(
        functools.partial(local, mesh.shape["seq"], mesh.shape["head"]),
        mesh=mesh,
        in_specs=(tokens, tokens, tokens, P("head", "seq"), weights, weights, weights, P("head")),
        out_specs=(tokens, weights, weights, weights),
        check_vma=False,
    )
```

```python
import functools
import math

import jax
import jax.numpy as jnp
from jax import lax
from jax.experimental import pallas as pl
from jax.experimental.pallas import tpu as pltpu
from jax.sharding import PartitionSpec as P

WINDOW = 512
EPS = 1e-06
TILE = 128
MESH = pl.DeviceIdType.MESH
F32 = jnp.float32
BF16 = jnp.bfloat16


def dot(a, b):
    return jnp.dot(a, b, preferred_element_type=F32)


def dot_lhs_t(a, b):
    return lax.dot_general(a, b, (((0,), (0,)), ((), ())), preferred_element_type=F32)


def dot_rhs_t(a, b):
    return lax.dot_general(a, b, (((1,), (1,)), ((), ())), preferred_element_type=F32)


def kernel(
    n, hn,
    q, k, v, rate, gain, w1, w3, w2,
    mixed, o1, o3, o2,
    wg, ug, pg, rs_out, rs_in, wb_out, wf_out, wf_in, own, g_out, g_in, ratio_out, ratio_in,
    qx, kx, vx, eta_x, gv, hid, dab, attn, attn_out, attn_in, branch, f_out, f_in, sq, sq_in,
    ag_s, ag_r, rs_s, rs_r, au_s, au_r, x_s, x_r, halo_s, halo_r, f_s, f_r, sq_s, sq_r,
):
    rows, width = q.shape
    heads, shard, hd = w1.shape
    line = n // 2
    tiles = rows // TILE
    me = lax.axis_index("seq")
    hme = lax.axis_index("head")
    m = lax.div(me, 2)
    c = lax.rem(me, 2)
    oc = 1 - c
    partner = 2 * m + oc
    step_to = (1, -1)
    weights = (w1, w3, w2)

    def seq_at(b):
        return 2 * lax.rem(b + line, line) + c

    def lanes(i):
        return pl.ds(pl.multiple_of(i * hd, hd), hd)

    def block(i):
        return pl.ds(pl.multiple_of(i * rows, rows), rows)

    def after_halo(i):
        return pl.ds(pl.multiple_of(WINDOW + i * rows, TILE), rows)

    barrier = pltpu.get_barrier_semaphore()
    for s in (partner, seq_at(m + 1), seq_at(m - 1)):
        pl.semaphore_signal(barrier, inc=1, device_id={"seq": s}, device_id_type=MESH)
    for d in range(1, hn):
        pl.semaphore_signal(
            barrier, inc=1, device_id={"head": lax.rem(hme + d, hn)}, device_id_type=MESH
        )
    for j, w in enumerate(weights):
        wg[j, m, c] = w[c].astype(BF16)
        wb_out[j] = w[oc].astype(BF16)
        wf_out[j] = w[oc]
    pl.semaphore_wait(barrier, 3 + hn - 1)

    pending = []

    def start(copy, when=None):
        if when is None:
            copy.start()
        else:
            pl.when(when)(copy.start)
        pending.append((copy, when))

    def wait(copy, when):
        pl.when(when)(copy.wait_recv)

    def to_partner(i, src, dst):
        return pltpu.make_async_remote_copy(
            src_ref=src, dst_ref=dst, send_sem=x_s.at[i], recv_sem=x_r.at[i],
            device_id={"seq": partner}, device_id_type=MESH,
        )

    x_w = to_partner(0, wb_out, wg.at[:, m, c])
    x_k = to_partner(1, k.at[:, lanes(oc)], kx.at[after_halo(c)])
    x_v = to_partner(2, v.at[:, lanes(oc)], vx.at[after_halo(c)])
    x_e = to_partner(3, rate, eta_x.at[c])
    x_f = to_partner(4, wf_out, wf_in)
    x_q = to_partner(5, q.at[:, lanes(oc)], qx.at[block(c)])
    x_g = to_partner(6, g_out, g_in)
    x_a = to_partner(7, attn_out, attn_in)
    x_r_ = to_partner(8, ratio_out, ratio_in)
    for x in (x_w, x_k, x_v, x_e, x_f, x_q):
        start(x)

    def link(ss, rr, src, dst, d, j, s):
        return pltpu.make_async_remote_copy(
            src_ref=src, dst_ref=dst, send_sem=ss.at[d, j, s - 1], recv_sem=rr.at[d, j, s - 1],
            device_id={"seq": seq_at(m + step_to[d])}, device_id_type=MESH,
        )

    def ahead(d):
        return line - 1 - m if d == 0 else m

    def gather_copy(buf, ss, rr, d, j, s):
        b = lax.rem(m - step_to[d] * (s - 1) + line, line)
        return link(ss, rr, buf.at[j, b], buf.at[j, b], d, j, s)

    def gather_wait(buf, ss, rr, d, j, s):
        b = lax.rem(m - step_to[d] * s + line, line)
        wait(link(ss, rr, buf.at[j, b], buf.at[j, b], d, j, s), ahead(1 - d) >= s)

    def gather_send(buf, ss, rr, j, s):
        for d in range(2):
            if s > 1:
                gather_wait(buf, ss, rr, d, j, s - 1)
            start(
                gather_copy(buf, ss, rr, d, j, s),
                jnp.logical_and(ahead(d) >= 1, ahead(1 - d) >= s - 1),
            )

    def gather_finish(buf, ss, rr, j):
        for d in range(2):
            gather_wait(buf, ss, rr, d, j, line - 1)

    def reduce_copy(d, j, s):
        return link(rs_s, rs_r, rs_out.at[d, j, s - 1], rs_in.at[d, j, s - 1], d, j, s)

    def reduce_send(j, s):
        for d in range(2):
            target = line - s if d == 0 else s - 1
            copy = reduce_copy(d, j, s)
            active = target > m if d == 0 else target < m
            first = ahead(1 - d) == 0

            @pl.when(jnp.logical_and(active, first))
            def _():
                rs_out[d, j, s - 1] = pg[j, target].astype(BF16)

            @pl.when(jnp.logical_and(active, jnp.logical_not(first)))
            def _():
                copy.wait_recv()
                part = pg[j, target] + rs_in[d, j, s - 1].astype(F32)
                rs_out[d, j, s - 1] = part.astype(BF16)

            start(copy, active)

    def reduce_finish(j):
        own[j] = pg[j, m]
        for d in range(2):
            for s in range(1, line):
                target = line - s if d == 0 else s - 1

                @pl.when(target == m)
                def _():
                    reduce_copy(d, j, s).wait_recv()
                    own[j] = own[j] + rs_in[d, j, s - 1].astype(F32)

        g_out[j] = own[j, oc]
        upd = own[j, c] + weights[j][c]
        own[j, c] = upd
        ug[j, m, c] = upd.astype(BF16)
        ug[j, m, oc] = (own[j, oc] + wf_in[j]).astype(BF16)

    halo = [
        pltpu.make_async_remote_copy(
            src_ref=x.at[2 * rows:2 * rows + WINDOW], dst_ref=x.at[0:WINDOW],
            send_sem=halo_s.at[i], recv_sem=halo_r.at[i],
            device_id={"seq": seq_at(m + 1)}, device_id_type=MESH,
        )
        for i, x in enumerate((kx, vx))
    ]

    def column(row):
        return jnp.transpose(jnp.broadcast_to(row, (TILE, row.shape[1])))

    def full(buf, j):
        return buf[j].reshape(n * shard, hd)

    def gradients():
        @pl.loop(0, 2 * tiles)
        def _(i):
            at = pl.ds(pl.multiple_of(i * TILE, TILE), TILE)
            kt = kx[pl.ds(pl.multiple_of(WINDOW + i * TILE, TILE), TILE), :]
            gt = gv[at, :]
            a = dot(kt, full(wg, 0))
            b = dot(kt, full(wg, 1))
            back = dot_rhs_t(gt, full(wg, 2))
            g = jax.nn.sigmoid(a)
            ag = a * g
            hid[at, :] = (ag * b).astype(BF16)
            dab[0, at, :] = (back * b * g * (1.0 + a * (1.0 - g))).astype(BF16)
            dab[1, at, :] = (back * ag).astype(BF16)

    def product(j):
        if j == 2:
            g = dot_lhs_t(hid[...], gv[...])
        else:
            g = dot_lhs_t(kx[WINDOW:, :], dab[j])
        pg[j] = g.reshape(line, 2, shard, hd)

    def attention(b, out):
        span = WINDOW + TILE

        @pl.loop(0, tiles)
        def _(i):
            base = pl.multiple_of(b * rows + i * TILE, TILE)
            s = dot_rhs_t(qx[pl.ds(base, TILE), :], kx[pl.ds(base, span), :])
            s = s * (1.0 / math.sqrt(hd))
            r = lax.broadcasted_iota(jnp.int32, (TILE, span), 0)
            u = lax.broadcasted_iota(jnp.int32, (TILE, span), 1)
            ok = (u > r) & (u <= r + WINDOW) & (base + u + m * 2 * rows >= WINDOW)
            s = jnp.where(ok, s, -jnp.inf)
            e = jnp.exp(s - jnp.max(s, axis=1, keepdims=True))
            p = (e * (1.0 / jnp.sum(e, axis=1, keepdims=True))).astype(BF16)
            res = dot(p, vx[pl.ds(base, span), :])
            out[pl.ds(pl.multiple_of(i * TILE, TILE), TILE), :] = res.astype(out.dtype)

    def sum_squares(buf, j):
        x = full(buf, j).astype(F32)
        return jnp.sum(x * x, axis=0, keepdims=True)

    def f_copy(i):
        at = pl.ds(pl.multiple_of(i * TILE, TILE), TILE)
        return pltpu.make_async_remote_copy(
            src_ref=f_out.at[at], dst_ref=f_in.at[at], send_sem=f_s.at[i], recv_sem=f_r.at[i],
            device_id={"seq": partner}, device_id_type=MESH,
        )

    def flat(f):
        row_sq = jnp.broadcast_to(jnp.sum(f * f, axis=1, keepdims=True), (TILE, TILE))
        return jnp.transpose(row_sq)[:8]

    def apply_tile(i, b):
        qt = qx[pl.ds(pl.multiple_of(b * rows + i * TILE, TILE), TILE), :]
        a = dot(qt, full(ug, 0)) * ratio_out[0:1]
        g = dot(qt, full(ug, 1)) * ratio_out[1:2]
        hh = (a * jax.nn.sigmoid(a) * g).astype(BF16)
        return dot(hh, full(ug, 2)) * ratio_out[2:3]

    kx[after_halo(c), :] = k[:, lanes(c)]
    vx[after_halo(c), :] = v[:, lanes(c)]
    qx[block(c), :] = q[:, lanes(c)]
    eta_x[c] = rate[...]

    @pl.when(m == 0)
    def _():
        for dst in (kx, vx):
            dst[:WINDOW, :] = jnp.zeros((WINDOW, hd), BF16)

    order_w, order_g = (0, 1, 2), (2, 0, 1)
    x_w.wait_recv()
    for j in order_w:
        gather_send(wg, ag_s, ag_r, j, 1)
    for s in range(2, line):
        for j in order_w:
            gather_send(wg, ag_s, ag_r, j, s)
    for x in (x_k, x_v, x_e):
        x.wait_recv()
    for h in halo:
        start(h, m < line - 1)
    for b in range(2):
        eta = column(eta_x[b, pl.ds(c, 1), :])[:, :1]
        at = slice(b * rows, (b + 1) * rows)
        vb = vx[WINDOW + b * rows:WINDOW + (b + 1) * rows, :]
        gv[at, :] = (eta * vb.astype(F32)).astype(BF16)
    for j in order_w:
        gather_finish(wg, ag_s, ag_r, j)
    gradients()
    for j in order_g:
        product(j)
        reduce_send(j, 1)
    x_q.wait_recv()
    for h in halo:
        wait(h, m > 0)
    attention(oc, attn_out)
    start(x_a)
    for s in range(2, line):
        for j in order_g:
            reduce_send(j, s)
    x_f.wait_recv()
    for j in order_g:
        reduce_finish(j)
        gather_send(ug, au_s, au_r, j, 1)
    start(x_g)
    attention(c, attn)
    for j in range(3):
        ratio_out[j:j + 1] = jnp.sqrt(sum_squares(wg, j))
    for s in range(2, line):
        for j in order_g:
            gather_send(ug, au_s, au_r, j, s)
    for j in order_g:
        gather_finish(ug, au_s, au_r, j)
        ratio_out[j:j + 1] = ratio_out[j:j + 1] / jnp.sqrt(sum_squares(ug, j) + EPS)
    start(x_r_)

    @pl.loop(0, tiles)
    def _(i):
        f_out[pl.ds(pl.multiple_of(i * TILE, TILE), TILE), :] = apply_tile(i, oc).astype(BF16)
        f_copy(i).start()

    @pl.loop(0, tiles)
    def _(i):
        at = pl.ds(pl.multiple_of(i * TILE, TILE), TILE)
        f = apply_tile(i, c)
        branch[at, :] = f
        sq[:, at] = flat(f)

    x_r_.wait_recv()
    x_g.wait_recv()
    for j, (w, out) in enumerate(zip(weights, (o1, o3, o2))):
        out[c] = own[j, c] * ratio_out[j:j + 1]
        out[oc] = (w[oc] + g_in[j]) * ratio_in[j:j + 1]

    @pl.loop(0, tiles)
    def _(i):
        at = pl.ds(pl.multiple_of(i * TILE, TILE), TILE)
        f_copy(i).wait_recv()
        sq[:, at] = sq[:, at] + flat(f_in[at, :].astype(F32))

    mine = []
    for d in range(1, hn):
        copy = pltpu.make_async_remote_copy(
            src_ref=sq, dst_ref=sq_in.at[d - 1],
            send_sem=sq_s.at[d - 1], recv_sem=sq_r.at[d - 1],
            device_id={"head": lax.rem(hme + d, hn)}, device_id_type=MESH,
        )
        copy.start()
        mine.append(copy)
    for copy, when in pending:
        if when is None:
            copy.wait_send()
        else:
            pl.when(when)(copy.wait_send)

    @pl.loop(0, tiles)
    def _(i):
        f_copy(i).wait_send()

    x_a.wait_recv()
    total = sq[...]
    for d, copy in enumerate(mine):
        copy.wait_recv()
        total = total + sq_in[d]
    for copy in mine:
        copy.wait_send()
    sq[...] = lax.rsqrt(total * (1.0 / (hn * width)) + EPS)

    @pl.loop(0, tiles)
    def _(i):
        at = pl.ds(pl.multiple_of(i * TILE, TILE), TILE)
        inv = column(sq[0:1, at])[:, :1]
        mixed[at, lanes(c)] = (attn[at, :] + branch[at, :] * inv * gain[:, lanes(c)]).astype(BF16)
        other = f_in[at, :].astype(F32) * inv * gain[:, lanes(oc)]
        mixed[at, lanes(oc)] = (attn_in[at, :].astype(F32) + other).astype(BF16)


def local(n, hn, queries, keys, values, rate, fast_gate, fast_up, fast_down, out_gain):
    rows, width = queries.shape
    heads, shard, hd = fast_gate.shape
    line = n // 2
    piece = (3, shard, hd)
    dma = pltpu.SemaphoreType.DMA
    vmem = pl.BlockSpec(memory_space=pltpu.VMEM)
    return pl.pallas_call(
        functools.partial(kernel, n, hn),
        out_shape=(
            jax.ShapeDtypeStruct((rows, width), BF16),
            jax.ShapeDtypeStruct(fast_gate.shape, F32),
            jax.ShapeDtypeStruct(fast_up.shape, F32),
            jax.ShapeDtypeStruct(fast_down.shape, F32),
        ),
        in_specs=[vmem] * 8,
        out_specs=(vmem,) * 4,
        scratch_shapes=[
            pltpu.VMEM((3, line, 2, shard, hd), BF16),
            pltpu.VMEM((3, line, 2, shard, hd), BF16),
            pltpu.VMEM((3, line, 2, shard, hd), F32),
            pltpu.VMEM((2, 3, line - 1, 2, shard, hd), BF16),
            pltpu.VMEM((2, 3, line - 1, 2, shard, hd), BF16),
            pltpu.VMEM(piece, BF16),
            pltpu.VMEM(piece, F32),
            pltpu.VMEM(piece, F32),
            pltpu.VMEM((3, 2, shard, hd), F32),
            pltpu.VMEM(piece, F32),
            pltpu.VMEM(piece, F32),
            pltpu.VMEM((8, hd), F32),
            pltpu.VMEM((8, hd), F32),
            pltpu.VMEM((2 * rows, hd), BF16),
            pltpu.VMEM((WINDOW + 2 * rows, hd), BF16),
            pltpu.VMEM((WINDOW + 2 * rows, hd), BF16),
            pltpu.VMEM((2,) + rate.shape, F32),
            pltpu.VMEM((2 * rows, hd), BF16),
            pltpu.VMEM((2 * rows, hd), BF16),
            pltpu.VMEM((2, 2 * rows, hd), BF16),
            pltpu.VMEM((rows, hd), F32),
            pltpu.VMEM((rows, hd), BF16),
            pltpu.VMEM((rows, hd), BF16),
            pltpu.VMEM((rows, hd), F32),
            pltpu.VMEM((rows, hd), BF16),
            pltpu.VMEM((rows, hd), BF16),
            pltpu.VMEM((8, rows), F32),
            pltpu.VMEM((hn - 1, 8, rows), F32),
        ]
        + [dma((2, 3, line - 1))] * 6
        + [dma((9,))] * 2
        + [dma((2,))] * 2
        + [dma((rows // TILE,))] * 2
        + [dma((hn - 1,))] * 2,
        compiler_params=pltpu.CompilerParams(
            collective_id=0, has_side_effects=True, vmem_limit_bytes=60 * 1024 * 1024
        ),
        name="ttt_layer",
    )(queries, keys, values, rate, out_gain.reshape(1, width), fast_gate, fast_up, fast_down)


def solution(mesh):
    weights = P("head", "seq", None)
    tokens = P("seq", "head")
    return jax.shard_map(
        functools.partial(local, mesh.shape["seq"], mesh.shape["head"]),
        mesh=mesh,
        in_specs=(tokens, tokens, tokens, P("head", "seq"), weights, weights, weights, P("head")),
        out_specs=(tokens, weights, weights, weights),
        check_vma=False,
    )
```

```python
import functools
import math

import jax
import jax.numpy as jnp
from jax import lax
from jax.experimental import pallas as pl
from jax.experimental.pallas import tpu as pltpu
from jax.sharding import PartitionSpec as P

WINDOW = 512
EPS = 1e-06
TILE = 128
MESH = pl.DeviceIdType.MESH
F32 = jnp.float32
BF16 = jnp.bfloat16


def dot(a, b):
    return jnp.dot(a, b, preferred_element_type=F32)


def dot_lhs_t(a, b):
    return lax.dot_general(a, b, (((0,), (0,)), ((), ())), preferred_element_type=F32)


def dot_rhs_t(a, b):
    return lax.dot_general(a, b, (((1,), (1,)), ((), ())), preferred_element_type=F32)


def kernel(
    n, hn,
    q, k, v, rate, gain, w1, w3, w2,
    mixed, o1, o3, o2,
    wg, ug, pg, rs_out, rs_in, wb_out, wf_out, wf_in, own, g_out, g_in, ratio_out, ratio_in,
    qx, kx, vx, eta_x, gv, hid, dab, attn, attn_out, attn_in, branch, f_out, f_in, sq, sq_in,
    ag_s, ag_r, rs_s, rs_r, au_s, au_r, x_s, x_r, halo_s, halo_r, f_s, f_r, sq_s, sq_r,
):
    rows, width = q.shape
    heads, shard, hd = w1.shape
    line = n // 2
    tiles = rows // TILE
    me = lax.axis_index("seq")
    hme = lax.axis_index("head")
    m = lax.div(me, 2)
    c = lax.rem(me, 2)
    oc = 1 - c
    partner = 2 * m + oc
    step_to = (1, -1)
    weights = (w1, w3, w2)

    def seq_at(b):
        return 2 * lax.rem(b + line, line) + c

    def lanes(i):
        return pl.ds(pl.multiple_of(i * hd, hd), hd)

    def block(i):
        return pl.ds(pl.multiple_of(i * rows, rows), rows)

    def after_halo(i):
        return pl.ds(pl.multiple_of(WINDOW + i * rows, TILE), rows)

    barrier = pltpu.get_barrier_semaphore()
    for s in (partner, seq_at(m + 1), seq_at(m - 1)):
        pl.semaphore_signal(barrier, inc=1, device_id={"seq": s}, device_id_type=MESH)
    for d in range(1, hn):
        pl.semaphore_signal(
            barrier, inc=1, device_id={"head": lax.rem(hme + d, hn)}, device_id_type=MESH
        )
    for j, w in enumerate(weights):
        wg[j, m, c] = w[c].astype(BF16)
        wb_out[j] = w[oc].astype(BF16)
        wf_out[j] = w[oc]
    pl.semaphore_wait(barrier, 3 + hn - 1)

    pending = []

    def start(copy, when=None):
        if when is None:
            copy.start()
        else:
            pl.when(when)(copy.start)
        pending.append((copy, when))

    def wait(copy, when):
        pl.when(when)(copy.wait_recv)

    def to_partner(i, src, dst):
        return pltpu.make_async_remote_copy(
            src_ref=src, dst_ref=dst, send_sem=x_s.at[i], recv_sem=x_r.at[i],
            device_id={"seq": partner}, device_id_type=MESH,
        )

    x_w = to_partner(0, wb_out, wg.at[:, m, c])
    x_k = to_partner(1, k.at[:, lanes(oc)], kx.at[after_halo(c)])
    x_v = to_partner(2, v.at[:, lanes(oc)], vx.at[after_halo(c)])
    x_e = to_partner(3, rate, eta_x.at[c])
    x_f = to_partner(4, wf_out, wf_in)
    x_q = to_partner(5, q.at[:, lanes(oc)], qx.at[block(c)])
    x_g = to_partner(6, g_out, g_in)
    x_a = to_partner(7, attn_out, attn_in)
    x_r_ = to_partner(8, ratio_out, ratio_in)
    for x in (x_w, x_k, x_v, x_e, x_f, x_q):
        start(x)

    def link(ss, rr, src, dst, d, j, s):
        return pltpu.make_async_remote_copy(
            src_ref=src, dst_ref=dst, send_sem=ss.at[d, j, s - 1], recv_sem=rr.at[d, j, s - 1],
            device_id={"seq": seq_at(m + step_to[d])}, device_id_type=MESH,
        )

    def ahead(d):
        return line - 1 - m if d == 0 else m

    def gather_copy(buf, ss, rr, d, j, s):
        b = lax.rem(m - step_to[d] * (s - 1) + line, line)
        return link(ss, rr, buf.at[j, b], buf.at[j, b], d, j, s)

    def gather_wait(buf, ss, rr, d, j, s):
        b = lax.rem(m - step_to[d] * s + line, line)
        wait(link(ss, rr, buf.at[j, b], buf.at[j, b], d, j, s), ahead(1 - d) >= s)

    def gather_send(buf, ss, rr, j, s):
        for d in range(2):
            if s > 1:
                gather_wait(buf, ss, rr, d, j, s - 1)
            start(
                gather_copy(buf, ss, rr, d, j, s),
                jnp.logical_and(ahead(d) >= 1, ahead(1 - d) >= s - 1),
            )

    def gather_finish(buf, ss, rr, j):
        for d in range(2):
            gather_wait(buf, ss, rr, d, j, line - 1)

    def reduce_copy(d, j, s):
        return link(rs_s, rs_r, rs_out.at[d, j, s - 1], rs_in.at[d, j, s - 1], d, j, s)

    def reduce_send(j, s, near):
        for d in range(2):
            target = line - s if d == 0 else s - 1
            copy = reduce_copy(d, j, s)
            closer = ahead(1 - d) * 2 < line
            turn = closer if near else jnp.logical_not(closer)
            active = jnp.logical_and(turn, target > m if d == 0 else target < m)
            first = ahead(1 - d) == 0
            if near:

                @pl.when(jnp.logical_and(active, first))
                def _():
                    rs_out[d, j, s - 1] = pg[j, target].astype(BF16)

            @pl.when(jnp.logical_and(active, jnp.logical_not(first)))
            def _():
                copy.wait_recv()
                part = pg[j, target] + rs_in[d, j, s - 1].astype(F32)
                rs_out[d, j, s - 1] = part.astype(BF16)

            start(copy, active)

    def reduce_piece(j):
        for s in range(1, line + 1):
            if s < line:
                reduce_send(j, s, True)
            if s > 1:
                reduce_send(j, s - 1, False)

    def reduce_finish(j):
        own[j] = pg[j, m]
        for d in range(2):
            for s in range(1, line):
                target = line - s if d == 0 else s - 1

                @pl.when(target == m)
                def _():
                    reduce_copy(d, j, s).wait_recv()
                    own[j] = own[j] + rs_in[d, j, s - 1].astype(F32)

        g_out[j] = own[j, oc]
        upd = own[j, c] + weights[j][c]
        own[j, c] = upd
        ug[j, m, c] = upd.astype(BF16)
        ug[j, m, oc] = (own[j, oc] + wf_in[j]).astype(BF16)

    halo = [
        pltpu.make_async_remote_copy(
            src_ref=x.at[2 * rows:2 * rows + WINDOW], dst_ref=x.at[0:WINDOW],
            send_sem=halo_s.at[i], recv_sem=halo_r.at[i],
            device_id={"seq": seq_at(m + 1)}, device_id_type=MESH,
        )
        for i, x in enumerate((kx, vx))
    ]

    def column(row):
        return jnp.transpose(jnp.broadcast_to(row, (TILE, row.shape[1])))

    def full(buf, j):
        return buf[j].reshape(n * shard, hd)

    def gradients():
        @pl.loop(0, 2 * tiles)
        def _(i):
            at = pl.ds(pl.multiple_of(i * TILE, TILE), TILE)
            kt = kx[pl.ds(pl.multiple_of(WINDOW + i * TILE, TILE), TILE), :]
            gt = gv[at, :]
            a = dot(kt, full(wg, 0))
            b = dot(kt, full(wg, 1))
            back = dot_rhs_t(gt, full(wg, 2))
            g = jax.nn.sigmoid(a)
            ag = a * g
            hid[at, :] = (ag * b).astype(BF16)
            dab[0, at, :] = (back * b * g * (1.0 + a * (1.0 - g))).astype(BF16)
            dab[1, at, :] = (back * ag).astype(BF16)

    def product(j):
        if j == 2:
            g = dot_lhs_t(hid[...], gv[...])
        else:
            g = dot_lhs_t(kx[WINDOW:, :], dab[j])
        pg[j] = g.reshape(line, 2, shard, hd)

    def attention(b, out):
        span = WINDOW + TILE

        @pl.loop(0, tiles)
        def _(i):
            base = pl.multiple_of(b * rows + i * TILE, TILE)
            s = dot_rhs_t(qx[pl.ds(base, TILE), :], kx[pl.ds(base, span), :])
            s = s * (1.0 / math.sqrt(hd))
            r = lax.broadcasted_iota(jnp.int32, (TILE, span), 0)
            u = lax.broadcasted_iota(jnp.int32, (TILE, span), 1)
            ok = (u > r) & (u <= r + WINDOW) & (base + u + m * 2 * rows >= WINDOW)
            s = jnp.where(ok, s, -jnp.inf)
            e = jnp.exp(s - jnp.max(s, axis=1, keepdims=True))
            p = (e * (1.0 / jnp.sum(e, axis=1, keepdims=True))).astype(BF16)
            res = dot(p, vx[pl.ds(base, span), :])
            out[pl.ds(pl.multiple_of(i * TILE, TILE), TILE), :] = res.astype(out.dtype)

    def sum_squares(buf, j):
        x = full(buf, j).astype(F32)
        return jnp.sum(x * x, axis=0, keepdims=True)

    def f_copy(i):
        at = pl.ds(pl.multiple_of(i * TILE, TILE), TILE)
        return pltpu.make_async_remote_copy(
            src_ref=f_out.at[at], dst_ref=f_in.at[at], send_sem=f_s.at[i], recv_sem=f_r.at[i],
            device_id={"seq": partner}, device_id_type=MESH,
        )

    def flat(f):
        row_sq = jnp.broadcast_to(jnp.sum(f * f, axis=1, keepdims=True), (TILE, TILE))
        return jnp.transpose(row_sq)[:8]

    def apply_tile(i, b):
        qt = qx[pl.ds(pl.multiple_of(b * rows + i * TILE, TILE), TILE), :]
        a = dot(qt, full(ug, 0)) * ratio_out[0:1]
        g = dot(qt, full(ug, 1)) * ratio_out[1:2]
        hh = (a * jax.nn.sigmoid(a) * g).astype(BF16)
        return dot(hh, full(ug, 2)) * ratio_out[2:3]

    kx[after_halo(c), :] = k[:, lanes(c)]
    vx[after_halo(c), :] = v[:, lanes(c)]
    qx[block(c), :] = q[:, lanes(c)]
    eta_x[c] = rate[...]

    @pl.when(m == 0)
    def _():
        for dst in (kx, vx):
            dst[:WINDOW, :] = jnp.zeros((WINDOW, hd), BF16)

    order_w = (0, 1, 2)
    x_w.wait_recv()
    for j in order_w:
        gather_send(wg, ag_s, ag_r, j, 1)
    for s in range(2, line):
        for j in order_w:
            gather_send(wg, ag_s, ag_r, j, s)
    x_k.wait_recv()
    start(halo[0], m < line - 1)
    x_v.wait_recv()
    start(halo[1], jnp.logical_and(m < line - 1, m * 2 < line))
    x_e.wait_recv()
    for b in range(2):
        eta = column(eta_x[b, pl.ds(c, 1), :])[:, :1]
        at = slice(b * rows, (b + 1) * rows)
        vb = vx[WINDOW + b * rows:WINDOW + (b + 1) * rows, :]
        gv[at, :] = (eta * vb.astype(F32)).astype(BF16)
    for j in order_w:
        gather_finish(wg, ag_s, ag_r, j)
    gradients()

    def pass_on(j, s):
        if s < line:
            gather_send(ug, au_s, au_r, j, s)

    product(0)
    reduce_piece(0)
    product(1)
    reduce_piece(1)
    product(2)
    x_f.wait_recv()
    reduce_finish(0)
    pass_on(0, 1)
    reduce_piece(2)
    start(halo[1], jnp.logical_and(m < line - 1, m * 2 >= line))
    reduce_finish(1)
    pass_on(1, 1)
    pass_on(0, 2)
    reduce_finish(2)
    pass_on(2, 1)
    start(x_g)
    pass_on(1, 2)
    pass_on(0, 3)
    x_q.wait_recv()
    for h in halo:
        wait(h, m > 0)
    attention(oc, attn_out)
    start(x_a)
    pass_on(2, 2)
    pass_on(1, 3)
    attention(c, attn)
    for j in range(3):
        ratio_out[j:j + 1] = jnp.sqrt(sum_squares(wg, j))
    pass_on(2, 3)
    for s in range(4, line):
        for j in order_w:
            pass_on(j, s)
    for j in order_w:
        gather_finish(ug, au_s, au_r, j)
        ratio_out[j:j + 1] = ratio_out[j:j + 1] / jnp.sqrt(sum_squares(ug, j) + EPS)
    start(x_r_)

    @pl.loop(0, tiles)
    def _(i):
        f_out[pl.ds(pl.multiple_of(i * TILE, TILE), TILE), :] = apply_tile(i, oc).astype(BF16)
        f_copy(i).start()

    @pl.loop(0, tiles)
    def _(i):
        at = pl.ds(pl.multiple_of(i * TILE, TILE), TILE)
        f = apply_tile(i, c)
        branch[at, :] = f
        sq[:, at] = flat(f)

    x_r_.wait_recv()
    x_g.wait_recv()
    for j, (w, out) in enumerate(zip(weights, (o1, o3, o2))):
        out[c] = own[j, c] * ratio_out[j:j + 1]
        out[oc] = (w[oc] + g_in[j]) * ratio_in[j:j + 1]

    @pl.loop(0, tiles)
    def _(i):
        at = pl.ds(pl.multiple_of(i * TILE, TILE), TILE)
        f_copy(i).wait_recv()
        sq[:, at] = sq[:, at] + flat(f_in[at, :].astype(F32))

    mine = []
    for d in range(1, hn):
        copy = pltpu.make_async_remote_copy(
            src_ref=sq, dst_ref=sq_in.at[d - 1],
            send_sem=sq_s.at[d - 1], recv_sem=sq_r.at[d - 1],
            device_id={"head": lax.rem(hme + d, hn)}, device_id_type=MESH,
        )
        copy.start()
        mine.append(copy)
    for copy, when in pending:
        if when is None:
            copy.wait_send()
        else:
            pl.when(when)(copy.wait_send)

    @pl.loop(0, tiles)
    def _(i):
        f_copy(i).wait_send()

    x_a.wait_recv()
    total = sq[...]
    for d, copy in enumerate(mine):
        copy.wait_recv()
        total = total + sq_in[d]
    for copy in mine:
        copy.wait_send()
    sq[...] = lax.rsqrt(total * (1.0 / (hn * width)) + EPS)

    @pl.loop(0, tiles)
    def _(i):
        at = pl.ds(pl.multiple_of(i * TILE, TILE), TILE)
        inv = column(sq[0:1, at])[:, :1]
        mixed[at, lanes(c)] = (attn[at, :] + branch[at, :] * inv * gain[:, lanes(c)]).astype(BF16)
        other = f_in[at, :].astype(F32) * inv * gain[:, lanes(oc)]
        mixed[at, lanes(oc)] = (attn_in[at, :].astype(F32) + other).astype(BF16)


def local(n, hn, queries, keys, values, rate, fast_gate, fast_up, fast_down, out_gain):
    rows, width = queries.shape
    heads, shard, hd = fast_gate.shape
    line = n // 2
    piece = (3, shard, hd)
    dma = pltpu.SemaphoreType.DMA
    vmem = pl.BlockSpec(memory_space=pltpu.VMEM)
    return pl.pallas_call(
        functools.partial(kernel, n, hn),
        out_shape=(
            jax.ShapeDtypeStruct((rows, width), BF16),
            jax.ShapeDtypeStruct(fast_gate.shape, F32),
            jax.ShapeDtypeStruct(fast_up.shape, F32),
            jax.ShapeDtypeStruct(fast_down.shape, F32),
        ),
        in_specs=[vmem] * 8,
        out_specs=(vmem,) * 4,
        scratch_shapes=[
            pltpu.VMEM((3, line, 2, shard, hd), BF16),
            pltpu.VMEM((3, line, 2, shard, hd), BF16),
            pltpu.VMEM((3, line, 2, shard, hd), F32),
            pltpu.VMEM((2, 3, line - 1, 2, shard, hd), BF16),
            pltpu.VMEM((2, 3, line - 1, 2, shard, hd), BF16),
            pltpu.VMEM(piece, BF16),
            pltpu.VMEM(piece, F32),
            pltpu.VMEM(piece, F32),
            pltpu.VMEM((3, 2, shard, hd), F32),
            pltpu.VMEM(piece, F32),
            pltpu.VMEM(piece, F32),
            pltpu.VMEM((8, hd), F32),
            pltpu.VMEM((8, hd), F32),
            pltpu.VMEM((2 * rows, hd), BF16),
            pltpu.VMEM((WINDOW + 2 * rows, hd), BF16),
            pltpu.VMEM((WINDOW + 2 * rows, hd), BF16),
            pltpu.VMEM((2,) + rate.shape, F32),
            pltpu.VMEM((2 * rows, hd), BF16),
            pltpu.VMEM((2 * rows, hd), BF16),
            pltpu.VMEM((2, 2 * rows, hd), BF16),
            pltpu.VMEM((rows, hd), F32),
            pltpu.VMEM((rows, hd), BF16),
            pltpu.VMEM((rows, hd), BF16),
            pltpu.VMEM((rows, hd), F32),
            pltpu.VMEM((rows, hd), BF16),
            pltpu.VMEM((rows, hd), BF16),
            pltpu.VMEM((8, rows), F32),
            pltpu.VMEM((hn - 1, 8, rows), F32),
        ]
        + [dma((2, 3, line - 1))] * 6
        + [dma((9,))] * 2
        + [dma((2,))] * 2
        + [dma((rows // TILE,))] * 2
        + [dma((hn - 1,))] * 2,
        compiler_params=pltpu.CompilerParams(
            collective_id=0, has_side_effects=True, vmem_limit_bytes=60 * 1024 * 1024
        ),
        name="ttt_layer",
    )(queries, keys, values, rate, out_gain.reshape(1, width), fast_gate, fast_up, fast_down)


def solution(mesh):
    weights = P("head", "seq", None)
    tokens = P("seq", "head")
    return jax.shard_map(
        functools.partial(local, mesh.shape["seq"], mesh.shape["head"]),
        mesh=mesh,
        in_specs=(tokens, tokens, tokens, P("head", "seq"), weights, weights, weights, P("head")),
        out_specs=(tokens, weights, weights, weights),
        check_vma=False,
    )
```

```python
import functools
import math

import jax
import jax.numpy as jnp
from jax import lax
from jax.experimental import pallas as pl
from jax.experimental.pallas import tpu as pltpu
from jax.sharding import PartitionSpec as P

WINDOW = 512
EPS = 1e-06
TILE = 128
MESH = pl.DeviceIdType.MESH
F32 = jnp.float32
BF16 = jnp.bfloat16


def dot(a, b):
    return jnp.dot(a, b, preferred_element_type=F32)


def dot_lhs_t(a, b):
    return lax.dot_general(a, b, (((0,), (0,)), ((), ())), preferred_element_type=F32)


def dot_rhs_t(a, b):
    return lax.dot_general(a, b, (((1,), (1,)), ((), ())), preferred_element_type=F32)


def kernel(
    n, hn,
    q, k, v, rate, gain, w1, w3, w2,
    mixed, o1, o3, o2,
    wg, ug, pg, rs_out, rs_in, wb_out, wf_out, wf_in, own, g_out, g_in, ratio_out, ratio_in,
    qx, kx, vx, eta_x, gv, hid, dab, attn, attn_out, attn_in, branch, f_out, f_in, sq, sq_in,
    ag_s, ag_r, rs_s, rs_r, au_s, au_r, x_s, x_r, halo_s, halo_r, f_s, f_r, sq_s, sq_r,
):
    rows, width = q.shape
    heads, shard, hd = w1.shape
    line = n // 2
    tiles = rows // TILE
    me = lax.axis_index("seq")
    hme = lax.axis_index("head")
    m = lax.div(me, 2)
    c = lax.rem(me, 2)
    oc = 1 - c
    partner = 2 * m + oc
    step_to = (1, -1)
    weights = (w1, w3, w2)

    def seq_at(b):
        return 2 * lax.rem(b + line, line) + c

    def lanes(i):
        return pl.ds(pl.multiple_of(i * hd, hd), hd)

    def block(i):
        return pl.ds(pl.multiple_of(i * rows, rows), rows)

    def after_halo(i):
        return pl.ds(pl.multiple_of(WINDOW + i * rows, TILE), rows)

    barrier = pltpu.get_barrier_semaphore()
    for s in (partner, seq_at(m + 1), seq_at(m - 1)):
        pl.semaphore_signal(barrier, inc=1, device_id={"seq": s}, device_id_type=MESH)
    for d in range(1, hn):
        pl.semaphore_signal(
            barrier, inc=1, device_id={"head": lax.rem(hme + d, hn)}, device_id_type=MESH
        )
    for j, w in enumerate(weights):
        wg[j, m, c] = w[c].astype(BF16)
        wb_out[j] = w[oc].astype(BF16)
        wf_out[j] = w[oc]
    pl.semaphore_wait(barrier, 3 + hn - 1)

    pending = []

    def start(copy, when=None):
        if when is None:
            copy.start()
        else:
            pl.when(when)(copy.start)
        pending.append((copy, when))

    def wait(copy, when):
        pl.when(when)(copy.wait_recv)

    def to_partner(i, src, dst):
        return pltpu.make_async_remote_copy(
            src_ref=src, dst_ref=dst, send_sem=x_s.at[i], recv_sem=x_r.at[i],
            device_id={"seq": partner}, device_id_type=MESH,
        )

    x_w = to_partner(0, wb_out, wg.at[:, m, c])
    x_k = to_partner(1, k.at[:, lanes(oc)], kx.at[after_halo(c)])
    x_v = to_partner(2, v.at[:, lanes(oc)], vx.at[after_halo(c)])
    x_e = to_partner(3, rate, eta_x.at[c])
    x_f = to_partner(4, wf_out, wf_in)
    x_q = to_partner(5, q.at[:, lanes(oc)], qx.at[block(c)])
    x_g = to_partner(6, g_out, g_in)
    x_a = to_partner(7, attn_out, attn_in)
    x_r_ = to_partner(8, ratio_out, ratio_in)
    for x in (x_w, x_k, x_v, x_e, x_f, x_q):
        start(x)

    def link(ss, rr, src, dst, d, j, s):
        return pltpu.make_async_remote_copy(
            src_ref=src, dst_ref=dst, send_sem=ss.at[d, j, s - 1], recv_sem=rr.at[d, j, s - 1],
            device_id={"seq": seq_at(m + step_to[d])}, device_id_type=MESH,
        )

    def ahead(d):
        return line - 1 - m if d == 0 else m

    def gather_copy(buf, ss, rr, d, j, s):
        b = lax.rem(m - step_to[d] * (s - 1) + line, line)
        return link(ss, rr, buf.at[j, b], buf.at[j, b], d, j, s)

    def gather_wait(buf, ss, rr, d, j, s):
        b = lax.rem(m - step_to[d] * s + line, line)
        wait(link(ss, rr, buf.at[j, b], buf.at[j, b], d, j, s), ahead(1 - d) >= s)

    def gather_send(buf, ss, rr, j, s):
        for d in range(2):
            if s > 1:
                gather_wait(buf, ss, rr, d, j, s - 1)
            start(
                gather_copy(buf, ss, rr, d, j, s),
                jnp.logical_and(ahead(d) >= 1, ahead(1 - d) >= s - 1),
            )

    def gather_finish(buf, ss, rr, j):
        for d in range(2):
            gather_wait(buf, ss, rr, d, j, line - 1)

    def reduce_copy(d, j, s):
        return link(rs_s, rs_r, rs_out.at[d, j, s - 1], rs_in.at[d, j, s - 1], d, j, s)

    def reduce_send(j, s, near):
        for d in range(2):
            target = line - s if d == 0 else s - 1
            copy = reduce_copy(d, j, s)
            closer = ahead(1 - d) * 2 < line
            turn = closer if near else jnp.logical_not(closer)
            active = jnp.logical_and(turn, target > m if d == 0 else target < m)
            first = ahead(1 - d) == 0
            if near:

                @pl.when(jnp.logical_and(active, first))
                def _():
                    rs_out[d, j, s - 1] = pg[j, target].astype(BF16)

            @pl.when(jnp.logical_and(active, jnp.logical_not(first)))
            def _():
                copy.wait_recv()
                part = pg[j, target] + rs_in[d, j, s - 1].astype(F32)
                rs_out[d, j, s - 1] = part.astype(BF16)

            start(copy, active)

    def reduce_piece(j):
        for s in range(1, line + 1):
            if s < line:
                reduce_send(j, s, True)
            if s > 1:
                reduce_send(j, s - 1, False)

    def reduce_finish(j):
        own[j] = pg[j, m]
        for d in range(2):
            for s in range(1, line):
                target = line - s if d == 0 else s - 1

                @pl.when(target == m)
                def _():
                    reduce_copy(d, j, s).wait_recv()
                    own[j] = own[j] + rs_in[d, j, s - 1].astype(F32)

        g_out[j] = own[j, oc]
        upd = own[j, c] + weights[j][c]
        own[j, c] = upd
        ug[j, m, c] = upd.astype(BF16)
        ug[j, m, oc] = (own[j, oc] + wf_in[j]).astype(BF16)

    halo = [
        pltpu.make_async_remote_copy(
            src_ref=x.at[2 * rows:2 * rows + WINDOW], dst_ref=x.at[0:WINDOW],
            send_sem=halo_s.at[i], recv_sem=halo_r.at[i],
            device_id={"seq": seq_at(m + 1)}, device_id_type=MESH,
        )
        for i, x in enumerate((kx, vx))
    ]

    def column(row):
        return jnp.transpose(jnp.broadcast_to(row, (TILE, row.shape[1])))

    def full(buf, j):
        return buf[j].reshape(n * shard, hd)

    def gradients():
        @pl.loop(0, 2 * tiles)
        def _(i):
            at = pl.ds(pl.multiple_of(i * TILE, TILE), TILE)
            kt = kx[pl.ds(pl.multiple_of(WINDOW + i * TILE, TILE), TILE), :]
            gt = gv[at, :]
            a = dot(kt, full(wg, 0))
            b = dot(kt, full(wg, 1))
            back = dot_rhs_t(gt, full(wg, 2))
            g = jax.nn.sigmoid(a)
            ag = a * g
            hid[at, :] = (ag * b).astype(BF16)
            dab[0, at, :] = (back * b * g * (1.0 + a * (1.0 - g))).astype(BF16)
            dab[1, at, :] = (back * ag).astype(BF16)

    def product(j):
        if j == 2:
            g = dot_lhs_t(hid[...], gv[...])
        else:
            g = dot_lhs_t(kx[WINDOW:, :], dab[j])
        pg[j] = g.reshape(line, 2, shard, hd)

    def attention(b, out):
        span = WINDOW + TILE

        @pl.loop(0, tiles)
        def _(i):
            base = pl.multiple_of(b * rows + i * TILE, TILE)
            s = dot_rhs_t(qx[pl.ds(base, TILE), :], kx[pl.ds(base, span), :])
            s = s * (1.0 / math.sqrt(hd))
            r = lax.broadcasted_iota(jnp.int32, (TILE, span), 0)
            u = lax.broadcasted_iota(jnp.int32, (TILE, span), 1)
            ok = (u > r) & (u <= r + WINDOW) & (base + u + m * 2 * rows >= WINDOW)
            s = jnp.where(ok, s, -jnp.inf)
            e = jnp.exp(s - jnp.max(s, axis=1, keepdims=True))
            p = (e * (1.0 / jnp.sum(e, axis=1, keepdims=True))).astype(BF16)
            res = dot(p, vx[pl.ds(base, span), :])
            out[pl.ds(pl.multiple_of(i * TILE, TILE), TILE), :] = res.astype(out.dtype)

    def sum_squares(buf, j):
        x = full(buf, j).astype(F32)
        return jnp.sum(x * x, axis=0, keepdims=True)

    def f_copy(i):
        at = pl.ds(pl.multiple_of(i * TILE, TILE), TILE)
        return pltpu.make_async_remote_copy(
            src_ref=f_out.at[at], dst_ref=f_in.at[at], send_sem=f_s.at[i], recv_sem=f_r.at[i],
            device_id={"seq": partner}, device_id_type=MESH,
        )

    def flat(f):
        row_sq = jnp.broadcast_to(jnp.sum(f * f, axis=1, keepdims=True), (TILE, TILE))
        return jnp.transpose(row_sq)[:8]

    def apply_tile(i, b):
        qt = qx[pl.ds(pl.multiple_of(b * rows + i * TILE, TILE), TILE), :]
        a = dot(qt, full(ug, 0)) * ratio_out[0:1]
        g = dot(qt, full(ug, 1)) * ratio_out[1:2]
        hh = (a * jax.nn.sigmoid(a) * g).astype(BF16)
        return dot(hh, full(ug, 2)) * ratio_out[2:3]

    kx[after_halo(c), :] = k[:, lanes(c)]
    vx[after_halo(c), :] = v[:, lanes(c)]
    qx[block(c), :] = q[:, lanes(c)]
    eta_x[c] = rate[...]

    @pl.when(m == 0)
    def _():
        for dst in (kx, vx):
            dst[:WINDOW, :] = jnp.zeros((WINDOW, hd), BF16)

    order_w = (0, 1, 2)
    x_w.wait_recv()
    for j in order_w:
        gather_send(wg, ag_s, ag_r, j, 1)
    for s in range(2, line):
        for j in order_w:
            gather_send(wg, ag_s, ag_r, j, s)
    x_k.wait_recv()
    start(halo[0], m < line - 1)
    x_v.wait_recv()
    start(halo[1], m < line - 1)
    x_e.wait_recv()
    for b in range(2):
        eta = column(eta_x[b, pl.ds(c, 1), :])[:, :1]
        at = slice(b * rows, (b + 1) * rows)
        vb = vx[WINDOW + b * rows:WINDOW + (b + 1) * rows, :]
        gv[at, :] = (eta * vb.astype(F32)).astype(BF16)
    for j in order_w:
        gather_finish(wg, ag_s, ag_r, j)
    gradients()

    def pass_on(j, s):
        if s < line:
            gather_send(ug, au_s, au_r, j, s)

    product(0)
    reduce_piece(0)
    product(1)
    reduce_piece(1)
    product(2)
    x_f.wait_recv()
    reduce_finish(0)
    pass_on(0, 1)
    reduce_piece(2)
    reduce_finish(1)
    pass_on(1, 1)
    pass_on(0, 2)
    reduce_finish(2)
    pass_on(2, 1)
    start(x_g)
    pass_on(1, 2)
    pass_on(0, 3)
    x_q.wait_recv()
    for h in halo:
        wait(h, m > 0)
    attention(oc, attn_out)
    start(x_a)
    pass_on(2, 2)
    pass_on(1, 3)
    attention(c, attn)
    for j in range(3):
        ratio_out[j:j + 1] = jnp.sqrt(sum_squares(wg, j))
    pass_on(2, 3)
    for s in range(4, line):
        for j in order_w:
            pass_on(j, s)
    for j in order_w:
        gather_finish(ug, au_s, au_r, j)
        ratio_out[j:j + 1] = ratio_out[j:j + 1] / jnp.sqrt(sum_squares(ug, j) + EPS)
    start(x_r_)

    @pl.loop(0, tiles)
    def _(i):
        f_out[pl.ds(pl.multiple_of(i * TILE, TILE), TILE), :] = apply_tile(i, oc).astype(BF16)
        f_copy(i).start()

    @pl.loop(0, tiles)
    def _(i):
        at = pl.ds(pl.multiple_of(i * TILE, TILE), TILE)
        f = apply_tile(i, c)
        branch[at, :] = f
        sq[:, at] = flat(f)

    x_r_.wait_recv()
    x_g.wait_recv()
    for j, (w, out) in enumerate(zip(weights, (o1, o3, o2))):
        out[c] = own[j, c] * ratio_out[j:j + 1]
        out[oc] = (w[oc] + g_in[j]) * ratio_in[j:j + 1]

    @pl.loop(0, tiles)
    def _(i):
        at = pl.ds(pl.multiple_of(i * TILE, TILE), TILE)
        f_copy(i).wait_recv()
        sq[:, at] = sq[:, at] + flat(f_in[at, :].astype(F32))

    mine = []
    for d in range(1, hn):
        copy = pltpu.make_async_remote_copy(
            src_ref=sq, dst_ref=sq_in.at[d - 1],
            send_sem=sq_s.at[d - 1], recv_sem=sq_r.at[d - 1],
            device_id={"head": lax.rem(hme + d, hn)}, device_id_type=MESH,
        )
        copy.start()
        mine.append(copy)
    for copy, when in pending:
        if when is None:
            copy.wait_send()
        else:
            pl.when(when)(copy.wait_send)

    @pl.loop(0, tiles)
    def _(i):
        f_copy(i).wait_send()

    x_a.wait_recv()
    total = sq[...]
    for d, copy in enumerate(mine):
        copy.wait_recv()
        total = total + sq_in[d]
    for copy in mine:
        copy.wait_send()
    sq[...] = lax.rsqrt(total * (1.0 / (hn * width)) + EPS)

    @pl.loop(0, tiles)
    def _(i):
        at = pl.ds(pl.multiple_of(i * TILE, TILE), TILE)
        inv = column(sq[0:1, at])[:, :1]
        mixed[at, lanes(c)] = (attn[at, :] + branch[at, :] * inv * gain[:, lanes(c)]).astype(BF16)
        other = f_in[at, :].astype(F32) * inv * gain[:, lanes(oc)]
        mixed[at, lanes(oc)] = (attn_in[at, :].astype(F32) + other).astype(BF16)


def local(n, hn, queries, keys, values, rate, fast_gate, fast_up, fast_down, out_gain):
    rows, width = queries.shape
    heads, shard, hd = fast_gate.shape
    line = n // 2
    piece = (3, shard, hd)
    dma = pltpu.SemaphoreType.DMA
    vmem = pl.BlockSpec(memory_space=pltpu.VMEM)
    return pl.pallas_call(
        functools.partial(kernel, n, hn),
        out_shape=(
            jax.ShapeDtypeStruct((rows, width), BF16),
            jax.ShapeDtypeStruct(fast_gate.shape, F32),
            jax.ShapeDtypeStruct(fast_up.shape, F32),
            jax.ShapeDtypeStruct(fast_down.shape, F32),
        ),
        in_specs=[vmem] * 8,
        out_specs=(vmem,) * 4,
        scratch_shapes=[
            pltpu.VMEM((3, line, 2, shard, hd), BF16),
            pltpu.VMEM((3, line, 2, shard, hd), BF16),
            pltpu.VMEM((3, line, 2, shard, hd), F32),
            pltpu.VMEM((2, 3, line - 1, 2, shard, hd), BF16),
            pltpu.VMEM((2, 3, line - 1, 2, shard, hd), BF16),
            pltpu.VMEM(piece, BF16),
            pltpu.VMEM(piece, F32),
            pltpu.VMEM(piece, F32),
            pltpu.VMEM((3, 2, shard, hd), F32),
            pltpu.VMEM(piece, F32),
            pltpu.VMEM(piece, F32),
            pltpu.VMEM((8, hd), F32),
            pltpu.VMEM((8, hd), F32),
            pltpu.VMEM((2 * rows, hd), BF16),
            pltpu.VMEM((WINDOW + 2 * rows, hd), BF16),
            pltpu.VMEM((WINDOW + 2 * rows, hd), BF16),
            pltpu.VMEM((2,) + rate.shape, F32),
            pltpu.VMEM((2 * rows, hd), BF16),
            pltpu.VMEM((2 * rows, hd), BF16),
            pltpu.VMEM((2, 2 * rows, hd), BF16),
            pltpu.VMEM((rows, hd), F32),
            pltpu.VMEM((rows, hd), BF16),
            pltpu.VMEM((rows, hd), BF16),
            pltpu.VMEM((rows, hd), F32),
            pltpu.VMEM((rows, hd), BF16),
            pltpu.VMEM((rows, hd), BF16),
            pltpu.VMEM((8, rows), F32),
            pltpu.VMEM((hn - 1, 8, rows), F32),
        ]
        + [dma((2, 3, line - 1))] * 6
        + [dma((9,))] * 2
        + [dma((2,))] * 2
        + [dma((rows // TILE,))] * 2
        + [dma((hn - 1,))] * 2,
        compiler_params=pltpu.CompilerParams(
            collective_id=0, has_side_effects=True, vmem_limit_bytes=60 * 1024 * 1024
        ),
        name="ttt_layer",
    )(queries, keys, values, rate, out_gain.reshape(1, width), fast_gate, fast_up, fast_down)


def solution(mesh):
    weights = P("head", "seq", None)
    tokens = P("seq", "head")
    return jax.shard_map(
        functools.partial(local, mesh.shape["seq"], mesh.shape["head"]),
        mesh=mesh,
        in_specs=(tokens, tokens, tokens, P("head", "seq"), weights, weights, weights, P("head")),
        out_specs=(tokens, weights, weights, weights),
        check_vma=False,
    )
```
